32 devices in a mesh: groups: 2 (over y), seq: 4 (over z), head: 2 (over x), fsdp: 2 (over core).
Axes of the slice: x: 2, y: 2, z: 4, core: 2. Of those that a mesh axis runs over, the one named last changes fastest.
Arguments:
- residual_in: bfloat16 [16384, 2048], P(('groups', 'seq', 'fsdp'), 'head'), parts along dimension 0, may hold values from -6 to 6
- query_rows: bfloat16 [16384, 2048], P(('groups', 'seq', 'fsdp'), 'head'), parts along dimension 0, may hold values from -7 to 7
- key_rows: bfloat16 [16384, 2048], P(('groups', 'seq', 'fsdp'), 'head'), parts along dimension 0, may hold values from -7 to 7
- value_rows: bfloat16 [16384, 2048], P(('groups', 'seq', 'fsdp'), 'head'), parts along dimension 0, may hold values from -6 to 6
- bc_weight: bfloat16 [2048, 256], P(('head', 'fsdp')), may hold values from -0.125 to 0.125
- decay_rate: float32 [16384, 32], P(('groups', 'seq', 'fsdp'), 'head'), parts along dimension 0, may hold values from 0 to 0.8
- level_codes: int32 [16384, 18], P(('groups', 'seq', 'fsdp')), parts along dimension 0, may hold values from 0 to 255
- level_scale: float32 [18], replicated, may hold values from 0.05 to 1
- positions: int32 [16384], P(('groups', 'seq', 'fsdp')), parts along dimension 0, may hold values from 0 to 2047, as said below
- ssm_gain: float32 [2048], P('head'), may hold values from 0.25 to 1.75
Outputs:
- mixed_out: bfloat16 [16384, 2048], P(('groups', 'seq', 'fsdp'), 'head'), parts along dimension 0
The draws below stay inside these ranges and needn't reach their ends.
There are 2 independent parts, one for each index of `groups`. The reference program is written for one: setup_inputs(seed, part) draws one part's arguments, and reference() takes and returns one part's arrays. A program takes and returns all parts, laid end to end along the dimension named above; an argument that names none is the same for every part. Nothing has to cross between parts.
Inputs may be any that keep to these rules, and one draw needn't show every extreme that they name: positions[t] is 0 where a document begins (always at t = 0) and positions[t - 1] + 1 elsewhere.
All inputs are finite; a program needn't handle non-finite values.
Results may differ from the reference program's by a relative error of at most 0.008.
Values may be sent and summed in bfloat16 or wider, within the bound.
A program may use at most 64 MiB of HBM per device.

```python
import math
import jax
import jax.numpy as jnp
from jax import lax

D = 2048
ATT_HEADS = 16
SSM_HEADS = 32
HEAD_VALUES = 64
STATES = 128
WINDOW = 128
LEVELS = 18
TOK_DEV = 1024
TOKEN_TOTAL = 8192


def attention_pair(key):
    base_key = jax.random.fold_in(key, 501)
    key_collection = jax.random.split(base_key, 2)
    query_vals = jnp.clip(jax.random.normal(key_collection[0], (TOKEN_TOTAL, D), jnp.float32), -4.0, 4.0)
    key_vals = jnp.clip(jax.random.normal(key_collection[1], (TOKEN_TOTAL, D), jnp.float32), -4.0, 4.0)
    return (query_vals, key_vals)


def draw_query_rows(key, part):
    return attention_pair(key)[0].astype(jnp.bfloat16)


def draw_key_rows(key, part):
    return attention_pair(key)[1].astype(jnp.bfloat16)


def draw_decay_rate(key, part):
    base_key = jax.random.fold_in(key, 733)
    key_collection = jax.random.split(base_key, 9)
    fast_share = 0.5
    fast_heads = jax.random.uniform(key_collection[0], (SSM_HEADS,), jnp.float32) < fast_share
    fast_rate = jnp.exp(jax.random.uniform(key_collection[1], (SSM_HEADS,), jnp.float32, math.log(1.0 / 50.0), math.log(1.0 / 30.0)))
    slow_rate = jnp.exp(jax.random.uniform(key_collection[2], (SSM_HEADS,), jnp.float32, math.log(0.4), math.log(1.2))) / TOKEN_TOTAL
    head_decay_speed = jnp.where(fast_heads, fast_rate, slow_rate)
    block_total = TOKEN_TOTAL // TOK_DEV
    narrow_factor = jnp.exp(jax.random.uniform(key_collection[3], (block_total, SSM_HEADS), jnp.float32, math.log(0.5), math.log(2.0)))
    wide_factor = jnp.exp(jax.random.uniform(key_collection[7], (block_total, SSM_HEADS), jnp.float32, math.log(0.25), math.log(4.0)))
    block_multiplier = jnp.where(fast_heads[None, :], narrow_factor, wide_factor)
    block_multiplier = jnp.repeat(block_multiplier, TOK_DEV, axis=0)
    jaggedness = jax.random.uniform(key_collection[4], (TOKEN_TOTAL, SSM_HEADS), jnp.float32, 0.5, 1.5)
    leading_spike = jax.random.randint(key_collection[5], (1,), 0, TOKEN_TOTAL)
    trailing_spike = (leading_spike + 1 + jax.random.randint(key_collection[8], (1,), 0, TOKEN_TOTAL - 1)) % TOKEN_TOTAL
    spike_position = jnp.concatenate([leading_spike, trailing_spike])
    spike_length = jnp.concatenate([jnp.full((1,), math.log(2.0), jnp.float32), jax.random.uniform(key_collection[6], (1,), jnp.float32, 0.22, 0.69)])
    token_index = jnp.arange(TOKEN_TOTAL, dtype=jnp.int32)
    spike_events = jnp.sum(jnp.where(token_index[:, None] == spike_position[None, :], spike_length[None, :], 0.0), axis=1)
    return head_decay_speed[None, :] * block_multiplier * jaggedness + spike_events[:, None]


def draw_positions(key, part):
    base_key = jax.random.fold_in(key, 919)
    token_index = jnp.arange(TOKEN_TOTAL, dtype=jnp.int32)
    offset = TOK_DEV // 2
    random_marks = (jax.random.randint(base_key, (TOKEN_TOTAL,), 0, 2 * TOK_DEV) == 0) & (token_index >= offset + 2 * TOK_DEV)
    start_marks = random_marks | (token_index % (2 * TOK_DEV) == offset) | (token_index == 0)
    starts = jnp.where(start_marks, token_index, 0)
    return token_index - lax.cummax(starts, axis=0)


def touch_ends(entries, key, smallest, top_value):
    dims = entries.shape
    place = [jax.random.randint(jax.random.fold_in(key, axis), (), 0, dims[axis]) for axis in range(len(dims))]
    entries = entries.at[tuple(place)].set(smallest)
    longest = dims.index(max(dims))
    place[longest] = (place[longest] + 1) % dims[longest]
    return entries.at[tuple(place)].set(top_value)


def shard_levels(stream_key, shape, cuts, least, top_value):
    level = 1.0
    for dim, blocks in cuts:
        draws = jax.random.uniform(jax.random.fold_in(jax.random.fold_in(stream_key, 6), dim), (blocks,), jnp.float32, least / len(cuts), top_value / len(cuts))
        level = level * jnp.repeat(jnp.exp(draws), shape[dim] // blocks).reshape((-1,) + (1,) * (len(shape) - 1 - dim))
    return level


def normal_values(stream_key, dims, scale, most, cuts=(), kind=jnp.bfloat16):
    values = scale * jax.random.normal(stream_key, dims, jnp.float32)
    if cuts:
        values = values * shard_levels(stream_key, dims, cuts, -0.22, 0.18)
    return jnp.clip(values, -most, most).astype(kind)


def setup_inputs(seed: int = 0, part: int = 0) -> dict:
    keys = jax.random.split(jax.random.key(seed), 11)
    part_keys = jax.random.split(jax.random.fold_in(keys[10], part), 11)
    residual_in = normal_values(part_keys[0], (TOKEN_TOTAL, D), 1.0, 6.0, ((0, 8), (1, 2)))
    query_rows = draw_query_rows(jax.random.fold_in(jax.random.fold_in(keys[10], part), 71), part)
    key_rows = draw_key_rows(jax.random.fold_in(jax.random.fold_in(keys[10], part), 71), part)
    value_rows = normal_values(part_keys[3], (TOKEN_TOTAL, D), 1.0, 6.0, ((0, 8), (1, 2)))
    bc_weight = normal_values(keys[4], (D, 2 * STATES), D ** -0.5, 0.125, ((0, 4),))
    decay_rate = draw_decay_rate(jax.random.fold_in(jax.random.fold_in(keys[10], part), 71), part)
    level_codes = touch_ends(jax.random.randint(part_keys[6], (TOKEN_TOTAL, LEVELS), 0, 256), jax.random.fold_in(part_keys[6], 1), 0, 255).astype(jnp.int32)
    level_scale = jnp.clip(jnp.exp(jax.random.uniform(keys[7], (LEVELS,), jnp.float32, math.log(0.05), math.log(1.0))), 0.05, 1.0)
    positions = draw_positions(jax.random.fold_in(jax.random.fold_in(keys[10], part), 71), part)
    ssm_gain = jnp.clip(1.0 + 0.15 * jax.random.normal(keys[9], (D,), jnp.float32), 0.25, 1.75)
    return dict(residual_in=residual_in, query_rows=query_rows, key_rows=key_rows, value_rows=value_rows, bc_weight=bc_weight, decay_rate=decay_rate, level_codes=level_codes, level_scale=level_scale, positions=positions, ssm_gain=ssm_gain)


def attend_block(queries, keys_part, values_part, doc_pos, head_count):
    query_len = queries.shape[0]
    key_len = keys_part.shape[0]
    window_len = key_len - query_len
    shaped_q = queries.reshape(query_len, head_count, -1).astype(jnp.float32)
    shaped_k = keys_part.reshape(key_len, head_count, -1).astype(jnp.float32)
    shaped_v = values_part.reshape(key_len, head_count, -1).astype(jnp.float32)
    scores = jnp.einsum('qhd,khd->hqk', shaped_q, shaped_k) / math.sqrt(shaped_q.shape[2])
    query_idx = jnp.arange(query_len, dtype=jnp.int32)[:, None]
    key_idx = jnp.arange(key_len, dtype=jnp.int32)[None, :]
    distance = query_idx + window_len - key_idx
    visible = (distance >= 0) & (distance < window_len) & (distance <= doc_pos[:, None])
    masked = jnp.where(visible[None], scores, -jnp.inf)
    top_score = lax.optimization_barrier(jnp.max(masked, axis=2, keepdims=True))
    weights = jnp.exp(masked - top_score)
    probabilities = (weights / lax.optimization_barrier(jnp.sum(weights, axis=2, keepdims=True))).astype(jnp.bfloat16)
    return jnp.einsum('hqk,khd->qhd', probabilities.astype(jnp.float32), shaped_v).reshape(query_len, -1)

def reference(residual_in, query_rows, key_rows, value_rows, bc_weight, decay_rate, level_codes, level_scale, positions, ssm_gain):
    tokens, feature_count = residual_in.shape
    padding = jnp.zeros((WINDOW, feature_count), jnp.bfloat16)
    keys_all = jnp.concatenate([padding, key_rows], axis=0)
    values_all = jnp.concatenate([padding, value_rows], axis=0)

    def attend_at(index):
        start_row = index * WINDOW
        return attend_block(lax.dynamic_slice_in_dim(query_rows, start_row, WINDOW, 0), lax.dynamic_slice_in_dim(keys_all, start_row, 2 * WINDOW, 0), lax.dynamic_slice_in_dim(values_all, start_row, 2 * WINDOW, 0), lax.dynamic_slice_in_dim(positions, start_row, WINDOW, 0), ATT_HEADS)
    attended = lax.map(attend_at, jnp.arange(tokens // WINDOW, dtype=jnp.int32)).reshape(tokens, feature_count)
    hidden = (residual_in.astype(jnp.float32) + attended).astype(jnp.bfloat16)
    bc_full = jnp.dot(hidden, bc_weight, preferred_element_type=jnp.float32).astype(jnp.bfloat16)
    block_count = tokens // TOK_DEV
    b_blocks = bc_full[:, :STATES].reshape(block_count, TOK_DEV, STATES)
    c_blocks = bc_full[:, STATES:].reshape(block_count, TOK_DEV, STATES)
    values_h = hidden.reshape(block_count, TOK_DEV, SSM_HEADS, HEAD_VALUES)
    log_cum = -jnp.cumsum(decay_rate.reshape(block_count, TOK_DEV, SSM_HEADS), axis=1)
    log_end = log_cum[:, TOK_DEV - 1]
    scaled = (jnp.exp(log_end[:, None, :] - log_cum)[..., None] * values_h.astype(jnp.float32)).astype(jnp.bfloat16)
    states = jnp.einsum('jrn,jrhp->jnhp', b_blocks.astype(jnp.float32), scaled.astype(jnp.float32))
    prefix = jnp.cumsum(log_end, axis=0) - log_end
    span_log = prefix[:, None, :] - prefix[None, :, :] - log_end[None, :, :]
    block_idx = jnp.arange(block_count, dtype=jnp.int32)
    differ = jnp.bitwise_xor(block_idx[:, None], block_idx[None, :])
    cross_count = block_count.bit_length() - 1
    carried_list = []
    for bit_pos in range(cross_count):
        chosen = (block_idx[None, :] < block_idx[:, None]) & (differ >= 1 << bit_pos) & (differ < 2 << bit_pos)
        level_w = jnp.exp(jnp.where(chosen[:, :, None], span_log, -jnp.inf))
        carried_list.append(jnp.einsum('jih,inhp->jnhp', level_w, states, precision=lax.Precision.HIGHEST))
    carried = jnp.stack(carried_list, axis=1).astype(jnp.bfloat16)
    lambdas = (level_codes.astype(jnp.float32) * level_scale[None, :]).reshape(block_count, TOK_DEV, LEVELS)
    local_bits = TOK_DEV.bit_length() - 1
    token_index = jnp.arange(TOK_DEV, dtype=jnp.int32)
    xor_idx = jnp.bitwise_xor(token_index[:, None], token_index[None, :])
    causal = token_index[None, :] <= token_index[:, None]
    level_index = jnp.zeros((TOK_DEV, TOK_DEV), jnp.int32)
    for bit_pos in range(local_bits):
        level_index = level_index + (xor_idx >= 1 << bit_pos).astype(jnp.int32)

    def finish(operands):
        lam_blk, b_blk, c_blk, cum_blk, values_blk, carried_blk, hidden_blk = operands
        level_weight = jnp.take_along_axis(lam_blk, level_index, axis=1)
        gram_mat = jnp.dot(c_blk, b_blk.T, preferred_element_type=jnp.float32)
        shared = jnp.where(causal, gram_mat * level_weight, 0.0)
        cum_heads = cum_blk.T
        decay_mat = jnp.exp(jnp.where(causal[None], cum_heads[:, :, None] - cum_heads[:, None, :], -jnp.inf))
        mixing = (shared[None] * decay_mat).astype(jnp.bfloat16)
        intra_term = jnp.einsum('hts,shp->thp', mixing.astype(jnp.float32), values_blk.astype(jnp.float32))
        level_reads = jnp.einsum('rn,lnhp->rlhp', c_blk.astype(jnp.float32), carried_blk.astype(jnp.float32))
        lam_cross = lam_blk[:, local_bits + 1:local_bits + 1 + cross_count]
        cross_term = jnp.einsum('rl,rlhp->rhp', lam_cross, level_reads) * jnp.exp(cum_blk)[:, :, None]
        ssm_out = intra_term + cross_term
        inv_rms = lax.rsqrt(lax.optimization_barrier(jnp.mean(ssm_out * ssm_out, axis=2, keepdims=True)) + 1e-05)
        result = hidden_blk.astype(jnp.float32) + (ssm_out * inv_rms).reshape(TOK_DEV, -1) * ssm_gain[None, :]
        return result.astype(jnp.bfloat16)
    outputs = lax.map(finish, (lambdas, b_blocks, c_blocks, log_cum, values_h, carried, hidden.reshape(block_count, TOK_DEV, feature_count)))
    return outputs.reshape(tokens, feature_count)
```

```python
import functools
import math

import jax
import jax.numpy as jnp
from jax import lax
from jax.experimental import pallas as pl
from jax.experimental.pallas import tpu as pltpu
from jax.sharding import PartitionSpec as P

HEAD_DIM = 128
HEAD_VALUES = 64
STATES = 128
WINDOW = 128
CHUNK = 128
LOG2E = math.log2(math.e)
F32 = jnp.float32
BF16 = jnp.bfloat16


def iota(shape, axis):
    return lax.broadcasted_iota(jnp.int32, shape, axis)


def dot(a, b):
    return jnp.dot(a, b, preferred_element_type=F32)


def dot_nt(a, b):
    return lax.dot_general(a, b, (((1,), (1,)), ((), ())), preferred_element_type=F32)


def dot_tn(a, b):
    return lax.dot_general(a, b, (((0,), (0,)), ((), ())), preferred_element_type=F32)


def attention_kernel(q, kp, kc, vp, vc, ek, ev, pos, res, w, hid, part):
    first = pl.program_id(0) == 0
    width = q.shape[1]
    pos_col = jnp.broadcast_to(pos[0].astype(F32), (CHUNK, CHUNK)).T
    row = iota((CHUNK, CHUNK), 0)
    col = iota((CHUNK, CHUNK), 1)
    near = (row - col).astype(F32)
    far = near + float(WINDOW)
    mask_cur = jnp.where((near >= 0) & (near <= pos_col), 0.0, -jnp.inf)
    mask_prev = jnp.where((far < float(WINDOW)) & (far <= pos_col), 0.0, -jnp.inf)
    mask = jnp.concatenate([mask_prev, mask_cur], axis=1)
    scale = LOG2E / math.sqrt(HEAD_DIM)
    for h in range(width // HEAD_DIM):
        cols = slice(h * HEAD_DIM, (h + 1) * HEAD_DIM)
        k_prev = jnp.where(first, ek[:, cols], kp[:, cols])
        v_prev = jnp.where(first, ev[:, cols], vp[:, cols])
        keys = jnp.concatenate([k_prev, kc[:, cols]], axis=0)
        vals = jnp.concatenate([v_prev, vc[:, cols]], axis=0)
        s = dot_nt(q[:, cols], keys) + mask
        top = jnp.max(s, axis=1, keepdims=True)
        e = jnp.exp2((s - top) * scale)
        total = jnp.sum(e, axis=1, keepdims=True)
        att = dot(e.astype(BF16), vals) * (1.0 / total)
        hid[:, cols] = (res[:, cols].astype(F32) + att).astype(BF16)
    part[...] = dot(hid[...], w[...]).astype(BF16)


def attention(q, k, v, edge_k, edge_v, positions, res, w):
    rows, width = q.shape
    n = rows // CHUNK
    cur = pl.BlockSpec((CHUNK, width), lambda i: (i, 0))
    prev = pl.BlockSpec((CHUNK, width), lambda i: (jnp.maximum(i - 1, 0), 0))
    fixed = lambda a: pl.BlockSpec(a.shape, lambda i: (0,) * a.ndim)
    return pl.pallas_call(
        attention_kernel,
        grid=(n,),
        in_specs=[cur, prev, cur, prev, cur, fixed(edge_k), fixed(edge_v),
                  pl.BlockSpec((1, 1, CHUNK), lambda i: (i, 0, 0)), cur, fixed(w)],
        out_specs=[cur, pl.BlockSpec((CHUNK, w.shape[1]), lambda i: (i, 0))],
        out_shape=[jax.ShapeDtypeStruct((rows, width), BF16),
                   jax.ShapeDtypeStruct((rows, w.shape[1]), BF16)],
        name="window_attention",
    )(q, k, k, v, v, edge_k, edge_v, positions.reshape(n, 1, CHUNK), res, w)


def split2(x):
    hi = x.astype(BF16)
    lo = (x - hi.astype(F32)).astype(BF16)
    return jnp.concatenate([hi, lo], axis=1)


def spread_matrix(heads, width):
    same = iota((2 * heads, width), 0) % heads == iota((2 * heads, width), 1) // HEAD_VALUES
    return jnp.where(same, 1.0, 0.0).astype(BF16)


def chunk_decay(decay):
    tri = jnp.where(iota((CHUNK, CHUNK), 1) <= iota((CHUNK, CHUNK), 0), 1.0, 0.0)
    return jnp.dot(tri, decay * LOG2E, precision=lax.Precision.HIGHEST, preferred_element_type=F32)


def chunk_state(b, u, cum, spread):
    left = cum[CHUNK - 1 :, :] - cum
    scaled = dot(split2(jnp.exp2(-left)), spread) * u.astype(F32)
    return dot_tn(b, scaled.astype(BF16))


def state_kernel(hid, p0, p1, decay, spread, state, gone):
    @pl.when(pl.program_id(0) == 0)
    def _():
        state[...] = jnp.zeros_like(state)
        gone[...] = jnp.ones_like(gone)

    b = (p0[:, :STATES].astype(F32) + p1[:, :STATES].astype(F32)).astype(BF16)
    cum = chunk_decay(decay[...])
    d = dot(split2(jnp.exp2(-cum[CHUNK - 8 :, :])), spread[...])[7:8, :]
    state[...] = state[...] * d + chunk_state(b, hid[...], cum, spread[...])
    gone[...] = gone[...] * d


def block_state(hid, p0, p1, decay, spread):
    rows, width = hid.shape
    cur = lambda a: pl.BlockSpec((CHUNK, a.shape[1]), lambda i: (i, 0))
    fixed = lambda s: pl.BlockSpec(s, lambda i: (0, 0))
    return pl.pallas_call(
        state_kernel,
        grid=(rows // CHUNK,),
        in_specs=[cur(hid), cur(p0), cur(p1), cur(decay), fixed(spread.shape)],
        out_specs=[fixed((STATES, width)), fixed((1, width))],
        out_shape=[jax.ShapeDtypeStruct((STATES, width), F32), jax.ShapeDtypeStruct((1, width), F32)],
        name="block_state",
    )(hid, p0, p1, decay, spread)


def local_kernel(steps, hid, p0, p1, decay, codes, scale, spread, y, held):
    j = pl.program_id(0)
    width = hid.shape[1]
    pairs = width // CHUNK
    low_levels = CHUNK.bit_length()

    @pl.when(j == 0)
    def _():
        held[...] = jnp.zeros_like(held)

    bc = (p0[...].astype(F32) + p1[...].astype(F32)).astype(BF16)
    b, c = bc[:, :STATES], bc[:, STATES:]
    lam = codes[...].astype(F32) * scale[...]
    cum = chunk_decay(decay[...])
    cum_t = cum.T
    row = iota((CHUNK, CHUNK), 0)
    col = iota((CHUNK, CHUNK), 1)
    differ = row ^ col
    weight = jnp.broadcast_to(lam[:, 0:1], (CHUNK, CHUNK))
    for level in range(1, low_levels):
        weight = jnp.where(differ >= 1 << level - 1, lam[:, level : level + 1], weight)
    shared = jnp.where(col <= row, dot_nt(c, b) * weight, 0.0)
    c32 = c.astype(F32)
    reach = dot(split2(jnp.exp2(-cum)), spread[...])
    d = reach[CHUNK - 1 :, :]
    left_lane = iota((CHUNK, CHUNK), 1) < HEAD_VALUES
    if steps:
        reads = jnp.concatenate(
            [(c32 * lam[:, low_levels + s : low_levels + s + 1]).astype(BF16) for s in range(steps)], axis=1
        )
    for g in range(pairs):
        cols = slice(g * CHUNK, (g + 1) * CHUNK)
        u = hid[:, cols]
        zero = jnp.zeros_like(u)
        mixes = []
        for h in (2 * g, 2 * g + 1):
            gap = jnp.minimum(cum_t[h : h + 1, :] - cum[:, h : h + 1], 0.0)
            mixes.append((shared * jnp.exp2(gap)).astype(BF16))
        stack = jnp.concatenate([jnp.where(left_lane, u, zero), jnp.where(left_lane, zero, u)], axis=0)
        term = dot(jnp.concatenate(mixes, axis=1), stack)
        if steps:
            term += dot(reads, held[:, cols].astype(BF16)) * reach[:, cols]
        y[:, cols] = term
    if steps:
        total = chunk_state(b, hid[...], cum, spread[...])
        after = j + 1
        for s in range(steps):
            bit = (after >> s) & 1
            fresh = jnp.where((after & ((1 << s) - 1)) == 0, 1, 0)
            keep = (bit * (1 - fresh)).astype(F32)
            take = (bit * fresh).astype(F32)
            rows = slice(s * STATES, (s + 1) * STATES)
            moved = held[rows, :] * d
            held[rows, :] = moved * keep + total * take
            total += moved


def local_terms(hid, p0, p1, decay, codes, scale, spread):
    rows, width = hid.shape
    n = rows // CHUNK
    steps = n.bit_length() - 1
    cur = lambda a: pl.BlockSpec((CHUNK, a.shape[1]), lambda i: (i, 0))
    fixed = lambda s: pl.BlockSpec(s, lambda i: (0, 0))
    return pl.pallas_call(
        functools.partial(local_kernel, steps),
        grid=(n,),
        in_specs=[cur(hid), cur(p0), cur(p1), cur(decay), cur(codes), fixed(scale.shape), fixed(spread.shape)],
        out_specs=cur(hid),
        out_shape=jax.ShapeDtypeStruct((rows, width), F32),
        scratch_shapes=[pltpu.VMEM((max(steps, 1) * STATES, width), F32)],
        name="local_terms",
        cost_estimate=pl.CostEstimate(flops=2 * rows * width * 1024, bytes_accessed=8 * rows * width, transcendentals=0),
    )(hid, p0, p1, decay, codes, scale, spread)


def finish_kernel(first_level, cross, hid, p0, p1, decay, codes, scale, spread, y, carried, gain, out, past):
    width = hid.shape[1]

    @pl.when(pl.program_id(0) == 0)
    def _():
        past[...] = jnp.ones_like(past)

    lam = codes[...].astype(F32) * scale[...]
    cum = chunk_decay(decay[...])
    reach = dot(split2(jnp.exp2(-cum)), spread[...])
    c = (p0[:, STATES:].astype(F32) + p1[:, STATES:].astype(F32)).astype(BF16).astype(F32)
    reads = jnp.concatenate(
        [(c * lam[:, first_level + s : first_level + s + 1]).astype(BF16) for s in range(cross)], axis=1
    )
    side = (CHUNK, CHUNK)
    group = jnp.where(iota(side, 0) // HEAD_VALUES == iota(side, 1) // HEAD_VALUES, 1.0 / HEAD_VALUES, 0.0).astype(BF16)
    for g in range(width // CHUNK):
        cols = slice(g * CHUNK, (g + 1) * CHUNK)
        term = y[:, cols] + dot(reads, carried[:, cols]) * (reach[:, cols] * past[:, cols])
        mean = dot((term * term).astype(BF16), group)
        out[:, cols] = (
            hid[:, cols].astype(F32) + term * lax.rsqrt(mean + 1e-05) * gain[:, cols]
        ).astype(BF16)
    past[...] = past[...] * reach[CHUNK - 1 :, :]


def finish(first_level, cross, hid, p0, p1, decay, codes, scale, spread, y, carried, gain):
    rows, width = hid.shape
    cur = lambda a: pl.BlockSpec((CHUNK, a.shape[1]), lambda i: (i, 0))
    fixed = lambda s: pl.BlockSpec(s, lambda i: (0, 0))
    return pl.pallas_call(
        functools.partial(finish_kernel, first_level, cross),
        grid=(rows // CHUNK,),
        in_specs=[cur(hid), cur(p0), cur(p1), cur(decay), cur(codes), fixed(scale.shape), fixed(spread.shape),
                  cur(y), fixed(carried.shape), fixed(gain.shape)],
        out_specs=cur(hid),
        out_shape=jax.ShapeDtypeStruct((rows, width), BF16),
        scratch_shapes=[pltpu.VMEM((1, width), F32)],
        name="finish",
    )(hid, p0, p1, decay, codes, scale, spread, y, carried, gain)


def from_behind(x, axis, by):
    length = lax.axis_size(axis)
    pairs = [(i, i + by) for i in range(length) if 0 <= i + by < length]
    return lax.ppermute(x, axis, pairs)


def partner(x, axis, distance):
    return lax.ppermute(x, axis, [(i, i ^ 1 << distance) for i in range(lax.axis_size(axis))])


def gather_rows(x, axis):
    pos = lax.axis_index(axis)
    for bit in range(lax.axis_size(axis).bit_length() - 1):
        other = partner(x, axis, bit)
        upper = ((pos >> bit) & 1) == 1
        x = jnp.concatenate([jnp.where(upper, other, x), jnp.where(upper, x, other)], axis=0)
    return x


def body(
    residual_in,
    query_rows,
    key_rows,
    value_rows,
    bc_weight,
    decay_rate,
    level_codes,
    level_scale,
    positions,
    ssm_gain,
):
    row_count, width = residual_in.shape
    line = ("seq", "fsdp")
    edge_k, edge_v = from_behind((key_rows[row_count - WINDOW :], value_rows[row_count - WINDOW :]), line, 1)
    hid, part = attention(
        query_rows, key_rows, value_rows, edge_k, edge_v, positions, residual_in, gather_rows(bc_weight, "fsdp")
    )
    head_bits = lax.axis_size("head").bit_length() - 1
    for bit in range(head_bits - 1):
        other = partner(part, "head", bit)
        part = (part.astype(F32) + other.astype(F32)).astype(BF16)
    other = partner(part, "head", head_bits - 1) if head_bits else jnp.zeros_like(part)
    spread = spread_matrix(decay_rate.shape[1], width)
    scale = level_scale[None, :]
    state, gone = block_state(hid, part, other, decay_rate, spread)
    y = local_terms(hid, part, other, decay_rate, level_codes, scale, spread)
    shard_pos = lax.axis_index(line)
    cross = lax.axis_size(line).bit_length() - 1
    before = jnp.ones_like(gone)
    carried = []
    for bit in range(cross):
        other_state, other_gone = partner((state.astype(BF16), gone), line, bit)
        other_state = other_state.astype(F32)
        upper = ((shard_pos >> bit) & 1) == 1
        carried.append(jnp.where(upper, other_state * before, 0.0).astype(BF16))
        state = jnp.where(upper, other_state * gone + state, state * other_gone + other_state)
        before = jnp.where(upper, before * other_gone, before)
        gone = gone * other_gone
    local_bits = row_count.bit_length() - 1
    return finish(
        local_bits + 1, cross, hid, part, other, decay_rate, level_codes, scale, spread, y,
        jnp.concatenate(carried, axis=0), ssm_gain[None, :],
    )


def solution(mesh):
    in_specs = (
        P(("groups", "seq", "fsdp"), "head"),
        P(("groups", "seq", "fsdp"), "head"),
        P(("groups", "seq", "fsdp"), "head"),
        P(("groups", "seq", "fsdp"), "head"),
        P(("head", "fsdp"), None),
        P(("groups", "seq", "fsdp"), "head"),
        P(("groups", "seq", "fsdp"), None),
        P(),
        P(("groups", "seq", "fsdp")),
        P("head"),
    )
    out_specs = P(("groups", "seq", "fsdp"), "head")
    return jax.shard_map(body, mesh=mesh, in_specs=in_specs, out_specs=out_specs, check_vma=False)
```

```python
import functools
import math

import jax
import jax.numpy as jnp
from jax import lax
from jax.experimental import pallas as pl
from jax.experimental.pallas import tpu as pltpu
from jax.sharding import PartitionSpec as P

HEAD_DIM = 128
HEAD_VALUES = 64
STATES = 128
WINDOW = 128
CHUNK = 128
LOG2E = math.log2(math.e)
F32 = jnp.float32
BF16 = jnp.bfloat16


def iota(shape, axis):
    return lax.broadcasted_iota(jnp.int32, shape, axis)


def dot(a, b):
    return jnp.dot(a, b, preferred_element_type=F32)


def dot_nt(a, b):
    return lax.dot_general(a, b, (((1,), (1,)), ((), ())), preferred_element_type=F32)


def dot_tn(a, b):
    return lax.dot_general(a, b, (((0,), (0,)), ((), ())), preferred_element_type=F32)


def split2(x):
    hi = x.astype(BF16)
    lo = (x - hi.astype(F32)).astype(BF16)
    return jnp.concatenate([hi, lo], axis=1)


def spread_matrix(heads, width):
    same = iota((2 * heads, width), 0) % heads == iota((2 * heads, width), 1) // HEAD_VALUES
    return jnp.where(same, 1.0, 0.0).astype(BF16)


def chunk_spec(rows, width, shift=0):
    return pl.BlockSpec((rows, width), lambda i: (i + shift, 0))


def fixed(shape):
    return pl.BlockSpec(shape, lambda i: (0,) * len(shape))


def cost(flops, moved):
    return pl.CostEstimate(flops=flops, bytes_accessed=moved, transcendentals=0)


def prepare_kernel(count, decay, codes, scale, cum_ref, exps, lam_ref, weight_ref):
    row = iota((CHUNK, CHUNK), 0)
    col = iota((CHUNK, CHUNK), 1)
    tri = jnp.where(row <= col, 1.0, 0.0)
    differ = row ^ col
    for c in range(count):
        rows = slice(c * CHUNK, (c + 1) * CHUNK)
        cum = jnp.dot(
            decay[:, rows] * LOG2E, tri, precision=lax.Precision.HIGHEST, preferred_element_type=F32
        ).T
        left = cum[CHUNK - 1 :, :] - cum
        cum_ref[rows, :] = cum
        exps[rows, :] = jnp.concatenate([split2(jnp.exp2(-left)), split2(jnp.exp2(-cum))], axis=1)
        lam = codes[rows, :].astype(F32) * scale[...]
        lam_ref[rows, :] = lam
        weight = jnp.broadcast_to(lam[:, 0:1], (CHUNK, CHUNK))
        for level in range(1, CHUNK.bit_length()):
            weight = jnp.where(differ >= 1 << level - 1, lam[:, level : level + 1], weight)
        weight_ref[rows, :] = jnp.where(col <= row, weight, 0.0)


def prepare(decay_t, codes, scale, count):
    heads, rows = decay_t.shape
    tall = count * CHUNK
    shapes = [(rows, heads), (rows, 4 * heads), codes.shape, (rows, CHUNK)]
    return pl.pallas_call(
        functools.partial(prepare_kernel, count),
        grid=(rows // tall,),
        in_specs=[pl.BlockSpec((heads, tall), lambda i: (0, i)), chunk_spec(tall, codes.shape[1]), fixed(scale.shape)],
        out_specs=[chunk_spec(tall, a[1]) for a in shapes],
        out_shape=[jax.ShapeDtypeStruct(a, BF16 if n == 1 else F32) for n, a in enumerate(shapes)],
        name="prepare",
        cost_estimate=cost(rows * 20000, 12 * rows * CHUNK),
    )(decay_t, codes, scale)


def attention_kernel(count, edged, q, kp, k, vp, v, pos, res, w, hid, part):
    width = q.shape[1]
    row = iota((CHUNK, CHUNK), 0)
    col = iota((CHUNK, CHUNK), 1)
    near = (row - col).astype(F32)
    far = near + float(WINDOW)
    scale = LOG2E / math.sqrt(HEAD_DIM)
    first = pl.program_id(0) == 0
    for c in range(count):
        rows = slice(c * CHUNK, (c + 1) * CHUNK)
        pos_col = jnp.broadcast_to(pos[c].astype(F32), (CHUNK, CHUNK)).T
        mask_cur = jnp.where((near >= 0) & (near <= pos_col), 0.0, -jnp.inf)
        mask_prev = jnp.where((far < float(WINDOW)) & (far <= pos_col), 0.0, -jnp.inf)
        mask = jnp.concatenate([mask_prev, mask_cur], axis=1)
        for h in range(width // HEAD_DIM):
            cols = slice(h * HEAD_DIM, (h + 1) * HEAD_DIM)
            if c:
                both = slice((c - 1) * CHUNK, (c + 1) * CHUNK)
                keys, vals = k[both, cols], v[both, cols]
            else:
                k_prev, v_prev = kp[:, cols], vp[:, cols]
                if edged is not None:
                    k_prev = jnp.where(first, edged[0][:CHUNK, cols], k_prev)
                    v_prev = jnp.where(first, edged[0][CHUNK:, cols], v_prev)
                keys = jnp.concatenate([k_prev, k[rows, cols]], axis=0)
                vals = jnp.concatenate([v_prev, v[rows, cols]], axis=0)
            s = dot_nt(q[rows, cols], keys) + mask
            top = jnp.max(s, axis=1, keepdims=True)
            e = jnp.exp2((s - top) * scale)
            total = jnp.sum(e, axis=1, keepdims=True)
            att = dot(e.astype(BF16), vals) * (1.0 / total)
            hid[rows, cols] = (res[rows, cols].astype(F32) + att).astype(BF16)
        part[rows, :] = dot(hid[rows, :], w[...]).astype(BF16)


def edged_kernel(count, edge, *refs):
    attention_kernel(count, (edge,), *refs)


def attention(q, k, v, edge, positions, res, w, start, stop, count):
    rows, width = q.shape
    n = rows // CHUNK
    tall = count * CHUNK
    base = start // count
    cur = chunk_spec(tall, width, base)
    prev = pl.BlockSpec((CHUNK, width), lambda i: (jnp.maximum((i + base) * count - 1, 0), 0))
    specs = [cur, prev, cur, prev, cur,
             pl.BlockSpec((count, 1, CHUNK), lambda i: (i + base, 0, 0)), cur, fixed(w.shape)]
    args = (q, k, k, v, v, positions.reshape(n, 1, CHUNK), res, w)
    kernel = functools.partial(attention_kernel, count, None)
    if edge is not None:
        specs, args = [fixed(edge.shape)] + specs, (edge,) + args
        kernel = functools.partial(edged_kernel, count)
    out_rows = (stop - start) * CHUNK
    return pl.pallas_call(
        kernel,
        grid=((stop - start) // count,),
        in_specs=specs,
        out_specs=[chunk_spec(tall, width), chunk_spec(tall, w.shape[1])],
        out_shape=[jax.ShapeDtypeStruct((out_rows, width), BF16),
                   jax.ShapeDtypeStruct((out_rows, w.shape[1]), BF16)],
        name="window_attention",
        cost_estimate=cost(out_rows * width * 4000, 10 * out_rows * width),
    )(*args)


def chunk_state(b, u, exps, spread):
    scaled = dot(exps[:, : exps.shape[1] // 2], spread) * u.astype(F32)
    return dot_tn(b, scaled.astype(BF16))


def reach_of(exps, spread):
    return dot(exps[:, exps.shape[1] // 2 :], spread)


def state_kernel(count, hid, p0, p1, exps, spread, state, gone):
    @pl.when(pl.program_id(0) == 0)
    def _():
        state[...] = jnp.zeros_like(state)
        gone[...] = jnp.ones_like(gone)

    for c in range(count):
        rows = slice(c * CHUNK, (c + 1) * CHUNK)
        b = (p0[rows, :STATES].astype(F32) + p1[rows, :STATES].astype(F32)).astype(BF16)
        d = reach_of(exps[(c + 1) * CHUNK - 16 : (c + 1) * CHUNK, :], spread[...])[15:16, :]
        state[...] = state[...] * d + chunk_state(b, hid[rows, :], exps[rows, :], spread[...])
        gone[...] = gone[...] * d


def block_state(hid, p0, p1, exps, spread, start, count):
    rows, width = hid.shape
    tall = count * CHUNK
    base = start // count
    return pl.pallas_call(
        functools.partial(state_kernel, count),
        grid=(rows // tall,),
        in_specs=[chunk_spec(tall, width), chunk_spec(tall, p0.shape[1]), chunk_spec(tall, p1.shape[1]),
                  chunk_spec(tall, exps.shape[1], base), fixed(spread.shape)],
        out_specs=[fixed((STATES, width)), fixed((1, width))],
        out_shape=[jax.ShapeDtypeStruct((STATES, width), F32), jax.ShapeDtypeStruct((1, width), F32)],
        name="block_state",
        cost_estimate=cost(rows * width * 4000, 4 * rows * width),
    )(hid, p0, p1, exps, spread)


def local_kernel(count, inner, outer, hid, p0, p1, cum_ref, exps, lam_ref, weight, spread, given, y, held):
    i = pl.program_id(0)
    width = hid.shape[1]
    low_levels = CHUNK.bit_length()
    steps = inner + outer

    @pl.when(i == 0)
    def _():
        held[...] = jnp.zeros_like(held)
        if outer:
            held[inner * STATES : steps * STATES, :] = given[...]

    left_lane = iota((CHUNK, CHUNK), 1) < HEAD_VALUES
    for c in range(count):
        rows = slice(c * CHUNK, (c + 1) * CHUNK)
        bc = (p0[rows, :].astype(F32) + p1[rows, :].astype(F32)).astype(BF16)
        b, cc = bc[:, :STATES], bc[:, STATES:]
        cum = cum_ref[rows, :]
        lam = lam_ref[rows, :]
        cum_t = cum.T
        shared = dot_nt(cc, b) * weight[rows, :]
        c32 = cc.astype(F32)
        reach = reach_of(exps[rows, :], spread[...])
        d = reach[CHUNK - 1 :, :]
        if steps:
            reads = jnp.concatenate(
                [(c32 * lam[:, low_levels + s : low_levels + s + 1]).astype(BF16) for s in range(steps)], axis=1
            )
        for g in range(width // CHUNK):
            cols = slice(g * CHUNK, (g + 1) * CHUNK)
            u = hid[rows, cols]
            zero = jnp.zeros_like(u)
            mixes = []
            for h in (2 * g, 2 * g + 1):
                gap = jnp.minimum(cum_t[h : h + 1, :] - cum[:, h : h + 1], 0.0)
                mixes.append((shared * jnp.exp2(gap)).astype(BF16))
            stack = jnp.concatenate([jnp.where(left_lane, u, zero), jnp.where(left_lane, zero, u)], axis=0)
            term = dot(jnp.concatenate(mixes, axis=1), stack)
            if steps:
                term += dot(reads, held[: steps * STATES, cols].astype(BF16)) * reach[:, cols]
            y[rows, cols] = term
        if inner:
            total = chunk_state(b, hid[rows, :], exps[rows, :], spread[...])
        after = i * count + c + 1
        for s in range(steps):
            part = slice(s * STATES, (s + 1) * STATES)
            moved = held[part, :] * d
            if s == inner:
                held[part, :] = moved
                continue
            bit = (after >> s) & 1
            fresh = jnp.where((after & ((1 << s) - 1)) == 0, 1, 0)
            held[part, :] = moved * (bit * (1 - fresh)).astype(F32) + total * (bit * fresh).astype(F32)
            total += moved


def local_terms(hid, p0, p1, prepared, spread, given, start, count):
    rows, width = hid.shape
    cum, exps, lam, weight = prepared
    tall = count * CHUNK
    base = start // count
    inner = (rows // CHUNK).bit_length() - 1
    outer = 1 if start else 0
    return pl.pallas_call(
        functools.partial(local_kernel, count, inner, outer),
        grid=(rows // tall,),
        in_specs=[chunk_spec(tall, width), chunk_spec(tall, p0.shape[1]), chunk_spec(tall, p1.shape[1])]
        + [chunk_spec(tall, a.shape[1], base) for a in (cum, exps, lam, weight)]
        + [fixed(spread.shape), fixed(given.shape)],
        out_specs=chunk_spec(tall, width),
        out_shape=jax.ShapeDtypeStruct((rows, width), F32),
        scratch_shapes=[pltpu.VMEM((max(inner + outer, 1) * STATES, width), F32)],
        name="local_terms",
        cost_estimate=cost(rows * width * 6000, 8 * rows * width),
    )(hid, p0, p1, cum, exps, lam, weight, spread, given)


def finish_kernel(count, first_level, cross, hid, p0, p1, exps, lam_ref, spread, y, carried, gain, begin, *rest):
    out, past = rest[-2:]
    width = hid.shape[1]

    @pl.when(pl.program_id(0) == 0)
    def _():
        past[...] = begin[...]

    side = (CHUNK, CHUNK)
    group = jnp.where(iota(side, 0) // HEAD_VALUES == iota(side, 1) // HEAD_VALUES, 1.0 / HEAD_VALUES, 0.0).astype(BF16)
    for n in range(count):
        rows = slice(n * CHUNK, (n + 1) * CHUNK)
        lam = lam_ref[rows, :]
        reach = reach_of(exps[rows, :], spread[...])
        c = (p0[rows, STATES:].astype(F32) + p1[rows, STATES:].astype(F32)).astype(BF16).astype(F32)
        reads = jnp.concatenate(
            [(c * lam[:, first_level + s : first_level + s + 1]).astype(BF16) for s in range(cross)], axis=1
        )
        for g in range(width // CHUNK):
            cols = slice(g * CHUNK, (g + 1) * CHUNK)
            term = y[rows, cols] + dot(reads, carried[:, cols]) * (reach[:, cols] * past[:, cols])
            mean = dot((term * term).astype(BF16), group)
            out[rows, cols] = (
                hid[rows, cols].astype(F32) + term * lax.rsqrt(mean + 1e-05) * gain[:, cols]
            ).astype(BF16)
        past[...] = past[...] * reach[CHUNK - 1 :, :]


def finish(first_level, cross, hid, p0, p1, prepared, spread, y, carried, gain, begin, whole, start, count, row_count):
    rows, width = hid.shape
    cum, exps, lam, weight = prepared
    tall = count * CHUNK
    base = start // count
    specs = [chunk_spec(tall, width), chunk_spec(tall, p0.shape[1]), chunk_spec(tall, p1.shape[1]),
             chunk_spec(tall, exps.shape[1], base), chunk_spec(tall, lam.shape[1], base), fixed(spread.shape),
             chunk_spec(tall, width), fixed(carried.shape), fixed(gain.shape), fixed(begin.shape)]
    args = (hid, p0, p1, exps, lam, spread, y, carried, gain, begin)
    aliases = {}
    if whole is not None:
        aliases = {len(specs): 0}
        specs, args = specs + [pl.BlockSpec(memory_space=pl.ANY)], args + (whole,)
    return pl.pallas_call(
        functools.partial(finish_kernel, count, first_level, cross),
        grid=(rows // tall,),
        in_specs=specs,
        out_specs=chunk_spec(tall, width, base),
        out_shape=jax.ShapeDtypeStruct((row_count, width), BF16),
        scratch_shapes=[pltpu.VMEM((1, width), F32)],
        input_output_aliases=aliases,
        name="finish",
    )(*args)


def from_behind(x, axis, by):
    length = lax.axis_size(axis)
    pairs = [(i, i + by) for i in range(length) if 0 <= i + by < length]
    return lax.ppermute(x, axis, pairs)


def partner(x, axis, distance):
    return lax.ppermute(x, axis, [(i, i ^ 1 << distance) for i in range(lax.axis_size(axis))])


def gather_rows(x, axis):
    pos = lax.axis_index(axis)
    for bit in range(lax.axis_size(axis).bit_length() - 1):
        other = partner(x, axis, bit)
        upper = ((pos >> bit) & 1) == 1
        x = jnp.concatenate([jnp.where(upper, other, x), jnp.where(upper, x, other)], axis=0)
    return x


def body(
    residual_in,
    query_rows,
    key_rows,
    value_rows,
    bc_weight,
    decay_rate,
    level_codes,
    level_scale,
    positions,
    ssm_gain,
):
    row_count, width = residual_in.shape
    line = ("seq", "fsdp")
    chunks = row_count // CHUNK
    half = chunks // 2
    count = 2
    edge = from_behind(
        jnp.concatenate([key_rows[row_count - WINDOW :], value_rows[row_count - WINDOW :]], axis=0), line, 1
    )
    weight = gather_rows(bc_weight, "fsdp")
    spread = spread_matrix(decay_rate.shape[1], width)
    prepared = prepare(decay_rate.T, level_codes, level_scale[None, :], count)
    exps = prepared[1]
    head_bits = lax.axis_size("head").bit_length() - 1

    def exchange(part):
        for bit in range(head_bits - 1):
            other = partner(part, "head", bit)
            part = (part.astype(F32) + other.astype(F32)).astype(BF16)
        other = partner(part, "head", head_bits - 1) if head_bits else jnp.zeros_like(part)
        return part, other

    inputs = (query_rows, key_rows, value_rows)
    hid_b, part_b = attention(*inputs, None, positions, residual_in, weight, half, chunks, count)
    pair_b = exchange(part_b)
    hid_a, part_a = attention(*inputs, edge, positions, residual_in, weight, 0, half, count)
    pair_a = exchange(part_a)
    state_b, gone_b = block_state(hid_b, *pair_b, exps, spread, half, count)
    state_a, gone_a = block_state(hid_a, *pair_a, exps, spread, 0, count)
    y_b = local_terms(hid_b, *pair_b, prepared, spread, state_a, half, count)
    y_a = local_terms(hid_a, *pair_a, prepared, spread, state_a, 0, count)
    state = state_a * gone_b + state_b
    gone = gone_a * gone_b
    shard_pos = lax.axis_index(line)
    cross = lax.axis_size(line).bit_length() - 1
    before = jnp.ones_like(gone)
    carried = []
    for bit in range(cross):
        other_state, other_gone = partner((state.astype(BF16), gone), line, bit)
        other_state = other_state.astype(F32)
        upper = ((shard_pos >> bit) & 1) == 1
        carried.append(jnp.where(upper, other_state * before, 0.0).astype(BF16))
        state = jnp.where(upper, other_state * gone + state, state * other_gone + other_state)
        before = jnp.where(upper, before * other_gone, before)
        gone = gone * other_gone
    carried = jnp.concatenate(carried, axis=0)
    level = row_count.bit_length()
    gain = ssm_gain[None, :]
    ones = jnp.ones_like(gone)
    out = finish(level, cross, hid_a, *pair_a, prepared, spread, y_a, carried, gain, ones, None, 0, count, row_count)
    return finish(
        level, cross, hid_b, *pair_b, prepared, spread, y_b, carried, gain, gone_a, out, half, count, row_count
    )


def solution(mesh):
    in_specs = (
        P(("groups", "seq", "fsdp"), "head"),
        P(("groups", "seq", "fsdp"), "head"),
        P(("groups", "seq", "fsdp"), "head"),
        P(("groups", "seq", "fsdp"), "head"),
        P(("head", "fsdp"), None),
        P(("groups", "seq", "fsdp"), "head"),
        P(("groups", "seq", "fsdp"), None),
        P(),
        P(("groups", "seq", "fsdp")),
        P("head"),
    )
    out_specs = P(("groups", "seq", "fsdp"), "head")
    return jax.shard_map(body, mesh=mesh, in_specs=in_specs, out_specs=out_specs, check_vma=False)
```

```python
import functools
import math

import jax
import jax.numpy as jnp
from jax import lax
from jax.experimental import pallas as pl
from jax.experimental.pallas import tpu as pltpu
from jax.sharding import PartitionSpec as P

HEAD_DIM = 128
HEAD_VALUES = 64
STATES = 128
WINDOW = 128
CHUNK = 128
LOG2E = math.log2(math.e)
F32 = jnp.float32
BF16 = jnp.bfloat16


def iota(shape, axis):
    return lax.broadcasted_iota(jnp.int32, shape, axis)


def dot(a, b):
    return jnp.dot(a, b, preferred_element_type=F32)


def dot_nt(a, b):
    return lax.dot_general(a, b, (((1,), (1,)), ((), ())), preferred_element_type=F32)


def dot_tn(a, b):
    return lax.dot_general(a, b, (((0,), (0,)), ((), ())), preferred_element_type=F32)


def split2(x):
    hi = x.astype(BF16)
    lo = (x - hi.astype(F32)).astype(BF16)
    return jnp.concatenate([hi, lo], axis=1)


def spread_matrix(heads, width):
    same = iota((2 * heads, width), 0) % heads == iota((2 * heads, width), 1) // HEAD_VALUES
    return jnp.where(same, 1.0, 0.0).astype(BF16)


def chunk_spec(rows, width, shift=0):
    return pl.BlockSpec((rows, width), lambda i: (i + shift, 0))


def fixed(shape):
    return pl.BlockSpec(shape, lambda i: (0,) * len(shape))


def cost(flops, moved):
    return pl.CostEstimate(flops=flops, bytes_accessed=moved, transcendentals=0)


def prepare_kernel(count, decay, codes, scale, cum_ref, exps, lam_ref, weight_ref):
    row = iota((CHUNK, CHUNK), 0)
    col = iota((CHUNK, CHUNK), 1)
    tri = jnp.where(row <= col, 1.0, 0.0)
    differ = row ^ col
    for c in range(count):
        rows = slice(c * CHUNK, (c + 1) * CHUNK)
        cum = jnp.dot(
            decay[:, rows] * LOG2E, tri, precision=lax.Precision.HIGHEST, preferred_element_type=F32
        ).T
        left = cum[CHUNK - 1 :, :] - cum
        cum_ref[rows, :] = cum
        exps[rows, :] = jnp.concatenate([split2(jnp.exp2(-left)), split2(jnp.exp2(-cum))], axis=1)
        lam = codes[rows, :].astype(F32) * scale[...]
        lam_ref[rows, :] = lam
        weight = jnp.broadcast_to(lam[:, 0:1], (CHUNK, CHUNK))
        for level in range(1, CHUNK.bit_length()):
            weight = jnp.where(differ >= 1 << level - 1, lam[:, level : level + 1], weight)
        weight_ref[rows, :] = jnp.where(col <= row, weight, 0.0)


def prepare(decay_t, codes, scale, count):
    heads, rows = decay_t.shape
    tall = count * CHUNK
    shapes = [(rows, heads), (rows, 4 * heads), codes.shape, (rows, CHUNK)]
    return pl.pallas_call(
        functools.partial(prepare_kernel, count),
        grid=(rows // tall,),
        in_specs=[pl.BlockSpec((heads, tall), lambda i: (0, i)), chunk_spec(tall, codes.shape[1]), fixed(scale.shape)],
        out_specs=[chunk_spec(tall, a[1]) for a in shapes],
        out_shape=[jax.ShapeDtypeStruct(a, BF16 if n == 1 else F32) for n, a in enumerate(shapes)],
        name="prepare",
        cost_estimate=cost(rows * 20000, 12 * rows * CHUNK),
    )(decay_t, codes, scale)


def attention_kernel(count, edged, q, kp, k, vp, v, pos, res, w, hid, part):
    width = q.shape[1]
    row = iota((CHUNK, CHUNK), 0)
    col = iota((CHUNK, CHUNK), 1)
    near = (row - col).astype(F32)
    far = near + float(WINDOW)
    scale = LOG2E / math.sqrt(HEAD_DIM)
    first = pl.program_id(0) == 0
    for c in range(count):
        rows = slice(c * CHUNK, (c + 1) * CHUNK)
        pos_col = jnp.broadcast_to(pos[c].astype(F32), (CHUNK, CHUNK)).T
        mask_cur = jnp.where((near >= 0) & (near <= pos_col), 0.0, -jnp.inf)
        mask_prev = jnp.where((far < float(WINDOW)) & (far <= pos_col), 0.0, -jnp.inf)
        mask = jnp.concatenate([mask_prev, mask_cur], axis=1)
        heads = [slice(h * HEAD_DIM, (h + 1) * HEAD_DIM) for h in range(width // HEAD_DIM)]
        keys, vals = [], []
        for cols in heads:
            if c:
                both = slice((c - 1) * CHUNK, (c + 1) * CHUNK)
                keys.append(k[both, cols])
                vals.append(v[both, cols])
            else:
                k_prev, v_prev = kp[:, cols], vp[:, cols]
                if edged is not None:
                    k_prev = jnp.where(first, edged[0][:CHUNK, cols], k_prev)
                    v_prev = jnp.where(first, edged[0][CHUNK:, cols], v_prev)
                keys.append(jnp.concatenate([k_prev, k[rows, cols]], axis=0))
                vals.append(jnp.concatenate([v_prev, v[rows, cols]], axis=0))
        scores = [dot_nt(q[rows, cols], key) + mask for cols, key in zip(heads, keys)]
        tops = [jnp.max(s, axis=1, keepdims=True) for s in scores]
        raised = [jnp.exp2((s - top) * scale) for s, top in zip(scores, tops)]
        totals = [jnp.sum(e, axis=1, keepdims=True) for e in raised]
        sums = [dot(e.astype(BF16), val) for e, val in zip(raised, vals)]
        tiles = [
            (res[rows, cols].astype(F32) + att * (1.0 / total)).astype(BF16)
            for cols, att, total in zip(heads, sums, totals)
        ]
        hidden = jnp.concatenate(tiles, axis=1)
        hid[rows, :] = hidden
        part[rows, :] = dot(hidden, w[...]).astype(BF16)


def edged_kernel(count, edge, *refs):
    attention_kernel(count, (edge,), *refs)


def attention(q, k, v, edge, positions, res, w, start, stop, count):
    rows, width = q.shape
    n = rows // CHUNK
    tall = count * CHUNK
    base = start // count
    cur = chunk_spec(tall, width, base)
    prev = pl.BlockSpec((CHUNK, width), lambda i: (jnp.maximum((i + base) * count - 1, 0), 0))
    specs = [cur, prev, cur, prev, cur,
             pl.BlockSpec((count, 1, CHUNK), lambda i: (i + base, 0, 0)), cur, fixed(w.shape)]
    args = (q, k, k, v, v, positions.reshape(n, 1, CHUNK), res, w)
    kernel = functools.partial(attention_kernel, count, None)
    if edge is not None:
        specs, args = [fixed(edge.shape)] + specs, (edge,) + args
        kernel = functools.partial(edged_kernel, count)
    out_rows = (stop - start) * CHUNK
    return pl.pallas_call(
        kernel,
        grid=((stop - start) // count,),
        in_specs=specs,
        out_specs=[chunk_spec(tall, width), chunk_spec(tall, w.shape[1])],
        out_shape=[jax.ShapeDtypeStruct((out_rows, width), BF16),
                   jax.ShapeDtypeStruct((out_rows, w.shape[1]), BF16)],
        name="window_attention",
        cost_estimate=cost(out_rows * width * 4000, 10 * out_rows * width),
    )(*args)


def chunk_state(b, u, exps, spread):
    scaled = dot(exps[:, : exps.shape[1] // 2], spread) * u.astype(F32)
    return dot_tn(b, scaled.astype(BF16))


def reach_of(exps, spread):
    return dot(exps[:, exps.shape[1] // 2 :], spread)


def state_kernel(count, hid, p0, p1, exps, spread, state, gone):
    @pl.when(pl.program_id(0) == 0)
    def _():
        state[...] = jnp.zeros_like(state)
        gone[...] = jnp.ones_like(gone)

    for c in range(count):
        rows = slice(c * CHUNK, (c + 1) * CHUNK)
        b = (p0[rows, :STATES].astype(F32) + p1[rows, :STATES].astype(F32)).astype(BF16)
        d = reach_of(exps[(c + 1) * CHUNK - 16 : (c + 1) * CHUNK, :], spread[...])[15:16, :]
        state[...] = state[...] * d + chunk_state(b, hid[rows, :], exps[rows, :], spread[...])
        gone[...] = gone[...] * d


def block_state(hid, p0, p1, exps, spread, start, count):
    rows, width = hid.shape
    tall = count * CHUNK
    base = start // count
    return pl.pallas_call(
        functools.partial(state_kernel, count),
        grid=(rows // tall,),
        in_specs=[chunk_spec(tall, width), chunk_spec(tall, p0.shape[1]), chunk_spec(tall, p1.shape[1]),
                  chunk_spec(tall, exps.shape[1], base), fixed(spread.shape)],
        out_specs=[fixed((STATES, width)), fixed((1, width))],
        out_shape=[jax.ShapeDtypeStruct((STATES, width), F32), jax.ShapeDtypeStruct((1, width), F32)],
        name="block_state",
        cost_estimate=cost(rows * width * 4000, 4 * rows * width),
    )(hid, p0, p1, exps, spread)


def local_kernel(count, inner, outer, hid, p0, p1, cum_ref, exps, lam_ref, weight, spread, given, y, held):
    i = pl.program_id(0)
    width = hid.shape[1]
    low_levels = CHUNK.bit_length()
    steps = inner + outer

    @pl.when(i == 0)
    def _():
        held[...] = jnp.zeros_like(held)
        if outer:
            held[inner * STATES : steps * STATES, :] = given[...]

    left_lane = iota((CHUNK, CHUNK), 1) < HEAD_VALUES
    for c in range(count):
        rows = slice(c * CHUNK, (c + 1) * CHUNK)
        bc = (p0[rows, :].astype(F32) + p1[rows, :].astype(F32)).astype(BF16)
        b, cc = bc[:, :STATES], bc[:, STATES:]
        cum = cum_ref[rows, :]
        lam = lam_ref[rows, :]
        cum_t = cum.T
        shared = dot_nt(cc, b) * weight[rows, :]
        c32 = cc.astype(F32)
        reach = reach_of(exps[rows, :], spread[...])
        d = reach[CHUNK - 1 :, :]
        if steps:
            reads = jnp.concatenate(
                [(c32 * lam[:, low_levels + s : low_levels + s + 1]).astype(BF16) for s in range(steps)], axis=1
            )
        terms = []
        for g in range(width // CHUNK):
            cols = slice(g * CHUNK, (g + 1) * CHUNK)
            u = hid[rows, cols]
            zero = jnp.zeros_like(u)
            mixes = []
            for h in (2 * g, 2 * g + 1):
                gap = jnp.minimum(cum_t[h : h + 1, :] - cum[:, h : h + 1], 0.0)
                mixes.append((shared * jnp.exp2(gap)).astype(BF16))
            stack = jnp.concatenate([jnp.where(left_lane, u, zero), jnp.where(left_lane, zero, u)], axis=0)
            terms.append(dot(jnp.concatenate(mixes, axis=1), stack))
        term = jnp.concatenate(terms, axis=1)
        if steps:
            term += dot(reads, held[: steps * STATES, :].astype(BF16)) * reach
        y[rows, :] = term
        if inner:
            total = chunk_state(b, hid[rows, :], exps[rows, :], spread[...])
        after = i * count + c + 1
        for s in range(steps):
            part = slice(s * STATES, (s + 1) * STATES)
            moved = held[part, :] * d
            if s == inner:
                held[part, :] = moved
                continue
            bit = (after >> s) & 1
            fresh = jnp.where((after & ((1 << s) - 1)) == 0, 1, 0)
            held[part, :] = moved * (bit * (1 - fresh)).astype(F32) + total * (bit * fresh).astype(F32)
            total += moved


def local_terms(hid, p0, p1, prepared, spread, given, start, count):
    rows, width = hid.shape
    cum, exps, lam, weight = prepared
    tall = count * CHUNK
    base = start // count
    inner = (rows // CHUNK).bit_length() - 1
    outer = 1 if start else 0
    return pl.pallas_call(
        functools.partial(local_kernel, count, inner, outer),
        grid=(rows // tall,),
        in_specs=[chunk_spec(tall, width), chunk_spec(tall, p0.shape[1]), chunk_spec(tall, p1.shape[1])]
        + [chunk_spec(tall, a.shape[1], base) for a in (cum, exps, lam, weight)]
        + [fixed(spread.shape), fixed(given.shape)],
        out_specs=chunk_spec(tall, width),
        out_shape=jax.ShapeDtypeStruct((rows, width), F32),
        scratch_shapes=[pltpu.VMEM((max(inner + outer, 1) * STATES, width), F32)],
        name="local_terms",
        cost_estimate=cost(rows * width * 6000, 8 * rows * width),
    )(hid, p0, p1, cum, exps, lam, weight, spread, given)


def finish_kernel(count, first_level, cross, hid, p0, p1, exps, lam_ref, spread, y, carried, gain, begin, *rest):
    out, past = rest[-2:]
    width = hid.shape[1]

    @pl.when(pl.program_id(0) == 0)
    def _():
        past[...] = begin[...]

    tile = min(2 * CHUNK, width)
    side = (tile, tile)
    group = jnp.where(iota(side, 0) // HEAD_VALUES == iota(side, 1) // HEAD_VALUES, 1.0 / HEAD_VALUES, 0.0).astype(BF16)
    lam = lam_ref[...]
    c = (p0[:, STATES:].astype(F32) + p1[:, STATES:].astype(F32)).astype(BF16).astype(F32)
    reads = jnp.concatenate(
        [(c * lam[:, first_level + s : first_level + s + 1]).astype(BF16) for s in range(cross)], axis=1
    )
    reach = reach_of(exps[...], spread[...])
    ahead = past[...]
    scaled = []
    for n in range(count):
        own = reach[n * CHUNK : (n + 1) * CHUNK, :]
        scaled.append(own * ahead)
        ahead = ahead * own[CHUNK - 1 :, :]
    past[...] = ahead
    scaled = jnp.concatenate(scaled, axis=0)
    tiles = [slice(g * tile, (g + 1) * tile) for g in range(width // tile)]
    terms = [y[:, cols] + dot(reads, carried[:, cols]) * scaled[:, cols] for cols in tiles]
    means = [dot((term * term).astype(BF16), group) for term in terms]
    results = [
        (hid[:, cols].astype(F32) + term * lax.rsqrt(mean + 1e-05) * gain[:, cols]).astype(BF16)
        for cols, term, mean in zip(tiles, terms, means)
    ]
    for cols, result in zip(tiles, results):
        out[:, cols] = result


def finish(first_level, cross, hid, p0, p1, prepared, spread, y, carried, gain, begin, whole, start, count, row_count):
    rows, width = hid.shape
    cum, exps, lam, weight = prepared
    tall = count * CHUNK
    base = start // count
    specs = [chunk_spec(tall, width), chunk_spec(tall, p0.shape[1]), chunk_spec(tall, p1.shape[1]),
             chunk_spec(tall, exps.shape[1], base), chunk_spec(tall, lam.shape[1], base), fixed(spread.shape),
             chunk_spec(tall, width), fixed(carried.shape), fixed(gain.shape), fixed(begin.shape)]
    args = (hid, p0, p1, exps, lam, spread, y, carried, gain, begin)
    aliases = {}
    if whole is not None:
        aliases = {len(specs): 0}
        specs, args = specs + [pl.BlockSpec(memory_space=pl.ANY)], args + (whole,)
    return pl.pallas_call(
        functools.partial(finish_kernel, count, first_level, cross),
        grid=(rows // tall,),
        in_specs=specs,
        out_specs=chunk_spec(tall, width, base),
        out_shape=jax.ShapeDtypeStruct((row_count, width), BF16),
        scratch_shapes=[pltpu.VMEM((1, width), F32)],
        input_output_aliases=aliases,
        name="finish",
    )(*args)


def from_behind(x, axis, by):
    length = lax.axis_size(axis)
    pairs = [(i, i + by) for i in range(length) if 0 <= i + by < length]
    return lax.ppermute(x, axis, pairs)


def partner(x, axis, distance):
    return lax.ppermute(x, axis, [(i, i ^ 1 << distance) for i in range(lax.axis_size(axis))])


def gather_rows(x, axis):
    pos = lax.axis_index(axis)
    for bit in range(lax.axis_size(axis).bit_length() - 1):
        other = partner(x, axis, bit)
        upper = ((pos >> bit) & 1) == 1
        x = jnp.concatenate([jnp.where(upper, other, x), jnp.where(upper, x, other)], axis=0)
    return x


def body(
    residual_in,
    query_rows,
    key_rows,
    value_rows,
    bc_weight,
    decay_rate,
    level_codes,
    level_scale,
    positions,
    ssm_gain,
):
    row_count, width = residual_in.shape
    line = ("seq", "fsdp")
    chunks = row_count // CHUNK
    half = chunks // 2
    count = 2
    edge = from_behind(
        jnp.concatenate([key_rows[row_count - WINDOW :], value_rows[row_count - WINDOW :]], axis=0), line, 1
    )
    weight = gather_rows(bc_weight, "fsdp")
    spread = spread_matrix(decay_rate.shape[1], width)
    prepared = prepare(decay_rate.T, level_codes, level_scale[None, :], count)
    exps = prepared[1]
    head_bits = lax.axis_size("head").bit_length() - 1

    def exchange(part):
        for bit in range(head_bits - 1):
            other = partner(part, "head", bit)
            part = (part.astype(F32) + other.astype(F32)).astype(BF16)
        other = partner(part, "head", head_bits - 1) if head_bits else jnp.zeros_like(part)
        return part, other

    inputs = (query_rows, key_rows, value_rows)
    hid_b, part_b = attention(*inputs, None, positions, residual_in, weight, half, chunks, count)
    pair_b = exchange(part_b)
    hid_a, part_a = attention(*inputs, edge, positions, residual_in, weight, 0, half, count)
    pair_a = exchange(part_a)
    state_b, gone_b = block_state(hid_b, *pair_b, exps, spread, half, count)
    state_a, gone_a = block_state(hid_a, *pair_a, exps, spread, 0, count)
    y_b = local_terms(hid_b, *pair_b, prepared, spread, state_a, half, count)
    y_a = local_terms(hid_a, *pair_a, prepared, spread, state_a, 0, count)
    state = state_a * gone_b + state_b
    gone = gone_a * gone_b
    shard_pos = lax.axis_index(line)
    cross = lax.axis_size(line).bit_length() - 1
    before = jnp.ones_like(gone)
    carried = []
    for bit in range(cross):
        other_state, other_gone = partner((state.astype(BF16), gone), line, bit)
        other_state = other_state.astype(F32)
        upper = ((shard_pos >> bit) & 1) == 1
        carried.append(jnp.where(upper, other_state * before, 0.0).astype(BF16))
        state = jnp.where(upper, other_state * gone + state, state * other_gone + other_state)
        before = jnp.where(upper, before * other_gone, before)
        gone = gone * other_gone
    carried = jnp.concatenate(carried, axis=0)
    level = row_count.bit_length()
    gain = ssm_gain[None, :]
    ones = jnp.ones_like(gone)
    out = finish(level, cross, hid_a, *pair_a, prepared, spread, y_a, carried, gain, ones, None, 0, count, row_count)
    return finish(
        level, cross, hid_b, *pair_b, prepared, spread, y_b, carried, gain, gone_a, out, half, count, row_count
    )


def solution(mesh):
    in_specs = (
        P(("groups", "seq", "fsdp"), "head"),
        P(("groups", "seq", "fsdp"), "head"),
        P(("groups", "seq", "fsdp"), "head"),
        P(("groups", "seq", "fsdp"), "head"),
        P(("head", "fsdp"), None),
        P(("groups", "seq", "fsdp"), "head"),
        P(("groups", "seq", "fsdp"), None),
        P(),
        P(("groups", "seq", "fsdp")),
        P("head"),
    )
    out_specs = P(("groups", "seq", "fsdp"), "head")
    return jax.shard_map(body, mesh=mesh, in_specs=in_specs, out_specs=out_specs, check_vma=False)
```

```python
import functools
import math

import jax
import jax.numpy as jnp
import numpy as np
from jax import lax
from jax.experimental import pallas as pl
from jax.experimental.pallas import tpu as pltpu
from jax.sharding import PartitionSpec as P

HEAD_DIM = 128
HEAD_VALUES = 64
STATES = 128
WINDOW = 128
CHUNK = 128
LOG2E = math.log2(math.e)
F32 = jnp.float32
BF16 = jnp.bfloat16


def iota(shape, axis):
    return lax.broadcasted_iota(jnp.int32, shape, axis)


def dot(a, b):
    return jnp.dot(a, b, preferred_element_type=F32)


def dot_nt(a, b):
    return lax.dot_general(a, b, (((1,), (1,)), ((), ())), preferred_element_type=F32)


def dot_tn(a, b):
    return lax.dot_general(a, b, (((0,), (0,)), ((), ())), preferred_element_type=F32)


def split2(x):
    hi = x.astype(BF16)
    lo = (x - hi.astype(F32)).astype(BF16)
    return jnp.concatenate([hi, lo], axis=1)


def spread_matrix(heads, width):
    same = np.arange(2 * heads)[:, None] % heads == np.arange(width)[None, :] // HEAD_VALUES
    return jnp.asarray(same.astype(np.float32), BF16)


def chunk_spec(rows, width, shift=0):
    return pl.BlockSpec((rows, width), lambda i: (i + shift, 0))


def fixed(shape):
    return pl.BlockSpec(shape, lambda i: (0,) * len(shape))


def cost(flops, moved):
    return pl.CostEstimate(flops=flops, bytes_accessed=moved, transcendentals=0)


def prepare_kernel(count, decay, codes, scale, cum_ref, exps, lam_ref, weight_ref):
    row = iota((CHUNK, CHUNK), 0)
    col = iota((CHUNK, CHUNK), 1)
    tri = jnp.where(row <= col, 1.0, 0.0)
    differ = row ^ col
    for c in range(count):
        rows = slice(c * CHUNK, (c + 1) * CHUNK)
        cum = jnp.dot(
            decay[:, rows] * LOG2E, tri, precision=lax.Precision.HIGHEST, preferred_element_type=F32
        ).T
        left = cum[CHUNK - 1 :, :] - cum
        cum_ref[rows, :] = cum
        exps[rows, :] = jnp.concatenate([split2(jnp.exp2(-left)), split2(jnp.exp2(-cum))], axis=1)
        lam = codes[rows, :].astype(F32) * scale[...]
        lam_ref[rows, :] = lam
        weight = jnp.broadcast_to(lam[:, 0:1], (CHUNK, CHUNK))
        for level in range(1, CHUNK.bit_length()):
            weight = jnp.where(differ >= 1 << level - 1, lam[:, level : level + 1], weight)
        weight_ref[rows, :] = jnp.where(col <= row, weight, 0.0)


def prepare(decay_t, codes, scale, count):
    heads, rows = decay_t.shape
    tall = count * CHUNK
    shapes = [(rows, heads), (rows, 4 * heads), codes.shape, (rows, CHUNK)]
    return pl.pallas_call(
        functools.partial(prepare_kernel, count),
        grid=(rows // tall,),
        in_specs=[pl.BlockSpec((heads, tall), lambda i: (0, i)), chunk_spec(tall, codes.shape[1]), fixed(scale.shape)],
        out_specs=[chunk_spec(tall, a[1]) for a in shapes],
        out_shape=[jax.ShapeDtypeStruct(a, BF16 if n == 1 else F32) for n, a in enumerate(shapes)],
        name="prepare",
        cost_estimate=cost(rows * 20000, 12 * rows * CHUNK),
    )(decay_t, codes, scale)


def attention_kernel(count, edged, q, kp, k, vp, v, pos, res, w, hid, part):
    width = q.shape[1]
    row = iota((CHUNK, CHUNK), 0)
    col = iota((CHUNK, CHUNK), 1)
    near = (row - col).astype(F32)
    far = near + float(WINDOW)
    scale = LOG2E / math.sqrt(HEAD_DIM)
    first = pl.program_id(0) == 0
    for c in range(count):
        rows = slice(c * CHUNK, (c + 1) * CHUNK)
        pos_col = jnp.broadcast_to(pos[c].astype(F32), (CHUNK, CHUNK)).T
        mask_cur = jnp.where((near >= 0) & (near <= pos_col), 0.0, -jnp.inf)
        mask_prev = jnp.where((far < float(WINDOW)) & (far <= pos_col), 0.0, -jnp.inf)
        mask = jnp.concatenate([mask_prev, mask_cur], axis=1)
        heads = [slice(h * HEAD_DIM, (h + 1) * HEAD_DIM) for h in range(width // HEAD_DIM)]
        keys, vals = [], []
        for cols in heads:
            if c:
                both = slice((c - 1) * CHUNK, (c + 1) * CHUNK)
                keys.append(k[both, cols])
                vals.append(v[both, cols])
            else:
                k_prev, v_prev = kp[:, cols], vp[:, cols]
                if edged is not None:
                    k_prev = jnp.where(first, edged[0][:CHUNK, cols], k_prev)
                    v_prev = jnp.where(first, edged[0][CHUNK:, cols], v_prev)
                keys.append(jnp.concatenate([k_prev, k[rows, cols]], axis=0))
                vals.append(jnp.concatenate([v_prev, v[rows, cols]], axis=0))
        scores = [dot_nt(q[rows, cols], key) + mask for cols, key in zip(heads, keys)]
        tops = [jnp.max(s, axis=1, keepdims=True) for s in scores]
        raised = [jnp.exp2((s - top) * scale) for s, top in zip(scores, tops)]
        totals = [jnp.sum(e, axis=1, keepdims=True) for e in raised]
        sums = [dot(e.astype(BF16), val) for e, val in zip(raised, vals)]
        tiles = [
            (res[rows, cols].astype(F32) + att * (1.0 / total)).astype(BF16)
            for cols, att, total in zip(heads, sums, totals)
        ]
        hidden = jnp.concatenate(tiles, axis=1)
        hid[rows, :] = hidden
        part[rows, :] = dot(hidden, w[...]).astype(BF16)


def edged_kernel(count, edge, *refs):
    attention_kernel(count, (edge,), *refs)


def attention(q, k, v, edge, positions, res, w, start, stop, count):
    rows, width = q.shape
    n = rows // CHUNK
    tall = count * CHUNK
    base = start // count
    cur = chunk_spec(tall, width, base)
    prev = pl.BlockSpec((CHUNK, width), lambda i: (jnp.maximum((i + base) * count - 1, 0), 0))
    specs = [cur, prev, cur, prev, cur,
             pl.BlockSpec((count, 1, CHUNK), lambda i: (i + base, 0, 0)), cur, fixed(w.shape)]
    args = (q, k, k, v, v, positions.reshape(n, 1, CHUNK), res, w)
    kernel = functools.partial(attention_kernel, count, None)
    if edge is not None:
        specs, args = [fixed(edge.shape)] + specs, (edge,) + args
        kernel = functools.partial(edged_kernel, count)
    out_rows = (stop - start) * CHUNK
    return pl.pallas_call(
        kernel,
        grid=((stop - start) // count,),
        in_specs=specs,
        out_specs=[chunk_spec(tall, width), chunk_spec(tall, w.shape[1])],
        out_shape=[jax.ShapeDtypeStruct((out_rows, width), BF16),
                   jax.ShapeDtypeStruct((out_rows, w.shape[1]), BF16)],
        name="window_attention",
        cost_estimate=cost(out_rows * width * 4000, 10 * out_rows * width),
    )(*args)


def chunk_state(b, u, exps, spread):
    scaled = dot(exps[:, : exps.shape[1] // 2], spread) * u.astype(F32)
    return dot_tn(b, scaled.astype(BF16))


def reach_of(exps, spread):
    return dot(exps[:, exps.shape[1] // 2 :], spread)


def state_kernel(count, hid, p0, p1, exps, spread, state, gone):
    @pl.when(pl.program_id(0) == 0)
    def _():
        state[...] = jnp.zeros_like(state)
        gone[...] = jnp.ones_like(gone)

    for c in range(count):
        rows = slice(c * CHUNK, (c + 1) * CHUNK)
        b = (p0[rows, :STATES].astype(F32) + p1[rows, :STATES].astype(F32)).astype(BF16)
        d = reach_of(exps[(c + 1) * CHUNK - 16 : (c + 1) * CHUNK, :], spread[...])[15:16, :]
        state[...] = state[...] * d + chunk_state(b, hid[rows, :], exps[rows, :], spread[...])
        gone[...] = gone[...] * d


def block_state(hid, p0, p1, exps, spread, start, count):
    rows, width = hid.shape
    tall = count * CHUNK
    base = start // count
    return pl.pallas_call(
        functools.partial(state_kernel, count),
        grid=(rows // tall,),
        in_specs=[chunk_spec(tall, width), chunk_spec(tall, p0.shape[1]), chunk_spec(tall, p1.shape[1]),
                  chunk_spec(tall, exps.shape[1], base), fixed(spread.shape)],
        out_specs=[fixed((STATES, width)), fixed((1, width))],
        out_shape=[jax.ShapeDtypeStruct((STATES, width), F32), jax.ShapeDtypeStruct((1, width), F32)],
        name="block_state",
        cost_estimate=cost(rows * width * 4000, 4 * rows * width),
    )(hid, p0, p1, exps, spread)


def local_kernel(count, inner, outer, hid, p0, p1, cum_ref, exps, lam_ref, weight, spread, given, y, held):
    i = pl.program_id(0)
    width = hid.shape[1]
    low_levels = CHUNK.bit_length()
    steps = inner + outer

    @pl.when(i == 0)
    def _():
        held[...] = jnp.zeros_like(held)
        if outer:
            held[inner * STATES : steps * STATES, :] = given[...]

    left_lane = iota((CHUNK, CHUNK), 1) < HEAD_VALUES
    for c in range(count):
        rows = slice(c * CHUNK, (c + 1) * CHUNK)
        bc = (p0[rows, :].astype(F32) + p1[rows, :].astype(F32)).astype(BF16)
        b, cc = bc[:, :STATES], bc[:, STATES:]
        cum = cum_ref[rows, :]
        lam = lam_ref[rows, :]
        cum_t = cum.T
        shared = dot_nt(cc, b) * weight[rows, :]
        c32 = cc.astype(F32)
        reach = reach_of(exps[rows, :], spread[...])
        d = reach[CHUNK - 1 :, :]
        if steps:
            reads = jnp.concatenate(
                [(c32 * lam[:, low_levels + s : low_levels + s + 1]).astype(BF16) for s in range(steps)], axis=1
            )
        terms = []
        for g in range(width // CHUNK):
            cols = slice(g * CHUNK, (g + 1) * CHUNK)
            u = hid[rows, cols]
            zero = jnp.zeros_like(u)
            mixes = []
            for h in (2 * g, 2 * g + 1):
                gap = jnp.minimum(cum_t[h : h + 1, :] - cum[:, h : h + 1], 0.0)
                mixes.append((shared * jnp.exp2(gap)).astype(BF16))
            stack = jnp.concatenate([jnp.where(left_lane, u, zero), jnp.where(left_lane, zero, u)], axis=0)
            terms.append(dot(jnp.concatenate(mixes, axis=1), stack))
        term = jnp.concatenate(terms, axis=1)
        if steps:
            term += dot(reads, held[: steps * STATES, :].astype(BF16)) * reach
        y[rows, :] = term
        if inner:
            total = chunk_state(b, hid[rows, :], exps[rows, :], spread[...])
        after = i * count + c + 1
        for s in range(steps):
            part = slice(s * STATES, (s + 1) * STATES)
            moved = held[part, :] * d
            if s == inner:
                held[part, :] = moved
                continue
            bit = (after >> s) & 1
            fresh = jnp.where((after & ((1 << s) - 1)) == 0, 1, 0)
            held[part, :] = moved * (bit * (1 - fresh)).astype(F32) + total * (bit * fresh).astype(F32)
            total += moved


def local_terms(hid, p0, p1, prepared, spread, given, start, count):
    rows, width = hid.shape
    cum, exps, lam, weight = prepared
    tall = count * CHUNK
    base = start // count
    inner = (rows // CHUNK).bit_length() - 1
    outer = 1 if start else 0
    return pl.pallas_call(
        functools.partial(local_kernel, count, inner, outer),
        grid=(rows // tall,),
        in_specs=[chunk_spec(tall, width), chunk_spec(tall, p0.shape[1]), chunk_spec(tall, p1.shape[1])]
        + [chunk_spec(tall, a.shape[1], base) for a in (cum, exps, lam, weight)]
        + [fixed(spread.shape), fixed(given.shape)],
        out_specs=chunk_spec(tall, width),
        out_shape=jax.ShapeDtypeStruct((rows, width), F32),
        scratch_shapes=[pltpu.VMEM((max(inner + outer, 1) * STATES, width), F32)],
        name="local_terms",
        cost_estimate=cost(rows * width * 6000, 8 * rows * width),
    )(hid, p0, p1, cum, exps, lam, weight, spread, given)


def finish_kernel(count, first_level, cross, hid, p0, p1, exps, lam_ref, spread, y, carried, gain, begin, *rest):
    out, past = rest[-2:]
    width = hid.shape[1]

    @pl.when(pl.program_id(0) == 0)
    def _():
        past[...] = begin[...]

    tile = min(2 * CHUNK, width)
    side = (tile, tile)
    group = jnp.where(iota(side, 0) // HEAD_VALUES == iota(side, 1) // HEAD_VALUES, 1.0 / HEAD_VALUES, 0.0).astype(BF16)
    lam = lam_ref[...]
    c = (p0[:, STATES:].astype(F32) + p1[:, STATES:].astype(F32)).astype(BF16).astype(F32)
    reads = jnp.concatenate(
        [(c * lam[:, first_level + s : first_level + s + 1]).astype(BF16) for s in range(cross)], axis=1
    )
    reach = reach_of(exps[...], spread[...])
    ahead = past[...]
    scaled = []
    for n in range(count):
        own = reach[n * CHUNK : (n + 1) * CHUNK, :]
        scaled.append(own * ahead)
        ahead = ahead * own[CHUNK - 1 :, :]
    past[...] = ahead
    scaled = jnp.concatenate(scaled, axis=0)
    tiles = [slice(g * tile, (g + 1) * tile) for g in range(width // tile)]
    terms = [y[:, cols] + dot(reads, carried[:, cols]) * scaled[:, cols] for cols in tiles]
    means = [dot((term * term).astype(BF16), group) for term in terms]
    results = [
        (hid[:, cols].astype(F32) + term * lax.rsqrt(mean + 1e-05) * gain[:, cols]).astype(BF16)
        for cols, term, mean in zip(tiles, terms, means)
    ]
    for cols, result in zip(tiles, results):
        out[:, cols] = result


def finish(first_level, cross, hid, p0, p1, prepared, spread, y, carried, gain, begin, whole, start, count, row_count):
    rows, width = hid.shape
    cum, exps, lam, weight = prepared
    tall = count * CHUNK
    base = start // count
    specs = [chunk_spec(tall, width), chunk_spec(tall, p0.shape[1]), chunk_spec(tall, p1.shape[1]),
             chunk_spec(tall, exps.shape[1], base), chunk_spec(tall, lam.shape[1], base), fixed(spread.shape),
             chunk_spec(tall, width), fixed(carried.shape), fixed(gain.shape), fixed(begin.shape)]
    args = (hid, p0, p1, exps, lam, spread, y, carried, gain, begin)
    aliases = {}
    if whole is not None:
        aliases = {len(specs): 0}
        specs, args = specs + [pl.BlockSpec(memory_space=pl.ANY)], args + (whole,)
    return pl.pallas_call(
        functools.partial(finish_kernel, count, first_level, cross),
        grid=(rows // tall,),
        in_specs=specs,
        out_specs=chunk_spec(tall, width, base),
        out_shape=jax.ShapeDtypeStruct((row_count, width), BF16),
        scratch_shapes=[pltpu.VMEM((1, width), F32)],
        input_output_aliases=aliases,
        name="finish",
    )(*args)


def from_behind(x, axis, by):
    length = lax.axis_size(axis)
    pairs = [(i, i + by) for i in range(length) if 0 <= i + by < length]
    return lax.ppermute(x, axis, pairs)


def partner(x, axis, distance):
    return lax.ppermute(x, axis, [(i, i ^ 1 << distance) for i in range(lax.axis_size(axis))])


def gather_rows(x, axis):
    pos = lax.axis_index(axis)
    for bit in range(lax.axis_size(axis).bit_length() - 1):
        other = partner(x, axis, bit)
        upper = ((pos >> bit) & 1) == 1
        x = jnp.concatenate([jnp.where(upper, other, x), jnp.where(upper, x, other)], axis=0)
    return x


def body(
    residual_in,
    query_rows,
    key_rows,
    value_rows,
    bc_weight,
    decay_rate,
    level_codes,
    level_scale,
    positions,
    ssm_gain,
):
    row_count, width = residual_in.shape
    line = ("seq", "fsdp")
    chunks = row_count // CHUNK
    half = chunks // 2
    count = 2
    edge = from_behind(
        jnp.concatenate([key_rows[row_count - WINDOW :], value_rows[row_count - WINDOW :]], axis=0), line, 1
    )
    weight = gather_rows(bc_weight, "fsdp")
    spread = spread_matrix(decay_rate.shape[1], width)
    prepared = prepare(decay_rate.T, level_codes, level_scale[None, :], half)
    exps = prepared[1]
    head_bits = lax.axis_size("head").bit_length() - 1

    def exchange(part):
        for bit in range(head_bits - 1):
            other = partner(part, "head", bit)
            part = (part.astype(F32) + other.astype(F32)).astype(BF16)
        other = partner(part, "head", head_bits - 1) if head_bits else jnp.zeros_like(part)
        return part, other

    inputs = (query_rows, key_rows, value_rows)
    hid_b, part_b = attention(*inputs, None, positions, residual_in, weight, half, chunks, count)
    pair_b = exchange(part_b)
    hid_a, part_a = attention(*inputs, edge, positions, residual_in, weight, 0, half, count)
    pair_a = exchange(part_a)
    state_b, gone_b = block_state(hid_b, *pair_b, exps, spread, half, half)
    state_a, gone_a = block_state(hid_a, *pair_a, exps, spread, 0, half)
    y_b = local_terms(hid_b, *pair_b, prepared, spread, state_a, half, count)
    y_a = local_terms(hid_a, *pair_a, prepared, spread, state_a, 0, count)
    state = state_a * gone_b + state_b
    gone = gone_a * gone_b
    shard_pos = lax.axis_index(line)
    cross = lax.axis_size(line).bit_length() - 1
    before = jnp.ones_like(gone)
    carried = []
    for bit in range(cross):
        other_state, other_gone = partner((state.astype(BF16), gone), line, bit)
        other_state = other_state.astype(F32)
        upper = ((shard_pos >> bit) & 1) == 1
        carried.append(jnp.where(upper, other_state * before, 0.0).astype(BF16))
        state = jnp.where(upper, other_state * gone + state, state * other_gone + other_state)
        before = jnp.where(upper, before * other_gone, before)
        gone = gone * other_gone
    carried = jnp.concatenate(carried, axis=0)
    level = row_count.bit_length()
    gain = ssm_gain[None, :]
    ones = jnp.asarray(np.ones(gone.shape, np.float32))
    out = finish(level, cross, hid_a, *pair_a, prepared, spread, y_a, carried, gain, ones, None, 0, count, row_count)
    return finish(
        level, cross, hid_b, *pair_b, prepared, spread, y_b, carried, gain, gone_a, out, half, count, row_count
    )


def solution(mesh):
    in_specs = (
        P(("groups", "seq", "fsdp"), "head"),
        P(("groups", "seq", "fsdp"), "head"),
        P(("groups", "seq", "fsdp"), "head"),
        P(("groups", "seq", "fsdp"), "head"),
        P(("head", "fsdp"), None),
        P(("groups", "seq", "fsdp"), "head"),
        P(("groups", "seq", "fsdp"), None),
        P(),
        P(("groups", "seq", "fsdp")),
        P("head"),
    )
    out_specs = P(("groups", "seq", "fsdp"), "head")
    return jax.shard_map(body, mesh=mesh, in_specs=in_specs, out_specs=out_specs, check_vma=False)
```
